32 devices in a mesh: stat: 16 (over z, x, core), tm: 2 (over y).
Axes of the slice: x: 2, y: 2, z: 4, core: 2. Of those that a mesh axis runs over, the one named last changes fastest.
Arguments:
- voltages: bfloat16 [2, 1024, 8, 4096], P(None, 'stat', 'tm'), may hold values from -6 to 6
- beam_weights: bfloat16 [2, 1024, 256], P(None, 'stat'), may hold values from -0.125 to 0.125
Outputs:
- beams: bfloat16 [4096, 8, 2, 256], P('stat', 'tm')
- visibilities: float32 [1024, 32, 2, 1024], P('tm', 'stat')
The draws below stay inside these ranges and needn't reach their ends.
All inputs are finite; a program needn't handle non-finite values.
Results may differ from the reference program's by a relative error of at most 0.011.
Values may be sent and summed in bfloat16 or wider, within the bound.
A program may use at most 64 MiB of HBM per device.

```python
import jax
import jax.numpy as jnp
from jax import lax

INPUTS = 1024
NA = 16
NB = 256
BEAMS = 256
AVG = 128
NF = 4096
SPEC = 8
VCH = 32
N_STAT = 16


def shard_levels(own_key, dims, cuts, low, largest):
    gain = 1.0
    for position, parts in cuts:
        draws = jax.random.uniform(jax.random.fold_in(jax.random.fold_in(own_key, 6), position), (parts,), jnp.float32, low / len(cuts), largest / len(cuts))
        gain = gain * jnp.repeat(jnp.exp(draws), dims[position] // parts).reshape((-1,) + (1,) * (len(dims) - 1 - position))
    return gain


def gaussian(stream_key, dims, scale, limit, shards=(), kind=jnp.bfloat16):
    level = shard_levels(stream_key, dims, shards, -0.22, 0.18) if shards else 1.0
    array = jax.random.normal(stream_key, dims, jnp.float32) * scale * level
    return jnp.minimum(jnp.maximum(array, -limit), limit).astype(kind)


def setup_inputs(seed: int = 0) -> dict:
    arg_keys = jax.random.split(jax.random.key(seed), 3)
    return {
        "voltages": gaussian(arg_keys[0], (2, INPUTS, SPEC, NF), 1.0, 6.0, ((1, 16), (2, 2))),
        "beam_weights": gaussian(arg_keys[1], (2, INPUTS, BEAMS), (2 * INPUTS) ** -0.5, 0.125, ((1, 16),)),
    }


def block_spectra(volt_block):
    signal = volt_block[0].astype(jnp.float32) + 1j * volt_block[1].astype(jnp.float32)
    transform = jnp.fft.fft(signal, axis=-1, norm="ortho")
    return jnp.stack([jnp.real(transform), jnp.imag(transform)]).astype(jnp.bfloat16)


def reference(voltages, beam_weights):
    block_width = INPUTS // N_STAT
    total_channels = NA * NB
    grouped = voltages.reshape(2, N_STAT, block_width, SPEC, total_channels).transpose(1, 0, 2, 3, 4)
    spectra = lax.map(block_spectra, grouped)
    weight_stack = jnp.stack([jnp.stack([beam_weights[0], beam_weights[1]], 1), jnp.stack([-beam_weights[1], beam_weights[0]], 1)], 0)
    weight_blocks = weight_stack.reshape(2, N_STAT, block_width, 2, BEAMS).transpose(1, 0, 2, 3, 4)

    def add_block(running, pair):
        spec_block, weight_block = pair
        partial_value = jnp.einsum('pisc,piqb->csqb', spec_block.astype(jnp.float32), weight_block.astype(jnp.float32))
        rounded = lax.optimization_barrier(partial_value.astype(jnp.bfloat16))
        return running + rounded.astype(jnp.float32), None

    beam_total, _ = lax.scan(add_block, jnp.zeros((total_channels, SPEC, 2, BEAMS), jnp.float32), (spectra, weight_blocks))
    beams = beam_total.astype(jnp.bfloat16)
    all_spectra = spectra.transpose(1, 0, 2, 3, 4).reshape(2, INPUTS, SPEC, total_channels)
    scale = 1.0 / (SPEC * AVG)

    def one_channel(channel_index):
        band = lax.dynamic_slice_in_dim(all_spectra, channel_index * AVG, AVG, 3).astype(jnp.float32)
        real_gram = jnp.einsum('pisc,pjsc->ij', band, band)
        mixed = jnp.einsum('isc,jsc->ij', band[1], band[0])
        return jnp.stack([real_gram, mixed - mixed.T]) * scale

    stacked = lax.map(one_channel, jnp.arange(VCH, dtype=jnp.int32))
    visibilities = stacked.transpose(2, 0, 1, 3)
    return beams, visibilities
```

```python
import functools
import math

import jax
import jax.numpy as jnp
import numpy as np
from jax import lax
from jax.experimental import pallas as pl
from jax.experimental.pallas import tpu as pltpu
from jax.sharding import PartitionSpec as P

NA = 16
NB = 256
AVG = 128


def dft_block(length):
    index = jnp.arange(length, dtype=jnp.int32)
    product = index[:, None] * index[None, :] % length
    angle = product.astype(jnp.float32) * (2.0 * math.pi / length)
    cosine = jnp.cos(angle)
    sine = jnp.sin(angle)
    return jnp.stack([jnp.stack([cosine, -sine]), jnp.stack([sine, cosine])])


def fine_spectra(voltages):
    block_inputs = voltages.shape[1]
    spectra_count = voltages.shape[2]
    signal = voltages.astype(jnp.float32).reshape(2, block_inputs, spectra_count, NA, NB)
    first = jnp.einsum("poak,pisab->osikb", dft_block(NA), signal, precision=lax.Precision.HIGH)
    outer_index = jnp.arange(NA, dtype=jnp.int32)
    inner_index = jnp.arange(NB, dtype=jnp.int32)
    rotation = (outer_index[:, None] * inner_index[None, :] % (NA * NB)).astype(jnp.float32) * (
        2.0 * math.pi / (NA * NB)
    )
    cos_twist = jnp.cos(rotation)
    sin_twist = jnp.sin(rotation)
    rotated = jnp.stack(
        [first[0] * cos_twist + first[1] * sin_twist, first[1] * cos_twist - first[0] * sin_twist]
    )
    final = jnp.einsum("osikb,ocbq->csiqk", rotated, dft_block(NB), precision=lax.Precision.HIGH)
    norm_factor = 1.0 / math.sqrt(NA * NB)
    return (
        (final * norm_factor).reshape(2, spectra_count, block_inputs, NA * NB).astype(jnp.bfloat16)
    )


def stack_weights(weights):
    return jnp.stack(
        [jnp.stack([weights[0], weights[1]], 1), jnp.stack([-weights[1], weights[0]], 1)], 0
    )


def body(voltages, beam_weights):
    stat_count = lax.axis_size("stat")
    time_count = lax.axis_size("tm")
    block_inputs = voltages.shape[1]
    spectra = fine_spectra(voltages)
    spectra_count = spectra.shape[1]
    channel_share = NA * NB // stat_count
    all_weights = lax.all_gather(beam_weights, "stat", axis=1, tiled=True)
    full_stack = stack_weights(all_weights)
    turned = lax.all_to_all(spectra, "stat", split_axis=3, concat_axis=2, tiled=True)
    item_count = turned.shape[1]

    def add_block(block_index, running):
        offset = (block_index * block_inputs).astype(jnp.int32)
        spec_block = lax.dynamic_slice_in_dim(turned, offset, block_inputs, 2)
        weight_block = lax.dynamic_slice_in_dim(full_stack, offset, block_inputs, 1)
        partial_value = jnp.einsum(
            "psic,piqb->csqb", spec_block, weight_block, preferred_element_type=jnp.float32
        )
        rounded = lax.optimization_barrier(partial_value.astype(jnp.bfloat16))
        return running + rounded.astype(jnp.float32)

    initial = jnp.zeros((turned.shape[3], item_count, 2, beam_weights.shape[2]), jnp.float32)
    beams = lax.fori_loop(0, stat_count, add_block, initial).astype(jnp.bfloat16)
    local_vch = channel_share // AVG
    scale = 1.0 / (spectra_count * time_count * AVG)
    split = turned.reshape(2, spectra_count, stat_count * block_inputs, local_vch, AVG)
    real_gram = jnp.einsum("psiva,psjva->ivj", split, split, preferred_element_type=jnp.float32)
    mixed = jnp.einsum("siva,sjva->ivj", split[1], split[0], preferred_element_type=jnp.float32)
    mixed = mixed - jnp.einsum(
        "siva,sjva->ivj", split[0], split[1], preferred_element_type=jnp.float32
    )
    visibilities = lax.psum_scatter(
        (jnp.stack([real_gram, mixed], axis=2) * scale).astype(jnp.bfloat16),
        "tm",
        scatter_dimension=0,
        tiled=True,
    ).astype(jnp.float32)
    return (beams, visibilities)

RADIX = 8


def dft_tables(points):
    inner = points // RADIX
    index = np.arange(inner)
    angle = 2.0 * np.pi * (index[:, None] * index[None, :] % inner) / inner
    scale = 1.0 / math.sqrt(points)
    matrix = np.concatenate([np.cos(angle), np.sin(angle)], 1) * scale
    turn = 2.0 * np.pi * (np.arange(RADIX)[:, None] * index[None, :]) / points
    return (
        jnp.asarray(matrix, jnp.bfloat16),
        jnp.asarray(np.cos(turn), jnp.float32),
        jnp.asarray(np.sin(turn), jnp.float32),
    )


def cadd(a, b):
    return a[0] + b[0], a[1] + b[1]


def csub(a, b):
    return a[0] - b[0], a[1] - b[1]


def times_minus_i(a):
    return a[1], -a[0]


def radix4(a):
    s02, d02 = cadd(a[0], a[2]), csub(a[0], a[2])
    s13, d13 = cadd(a[1], a[3]), times_minus_i(csub(a[1], a[3]))
    return [cadd(s02, s13), cadd(d02, d13), csub(s02, s13), csub(d02, d13)]


def radix8(a):
    even, odd = radix4(a[0::2]), radix4(a[1::2])
    root = math.sqrt(0.5)
    o1, o2, o3 = odd[1], times_minus_i(odd[2]), odd[3]
    o1 = ((o1[0] + o1[1]) * root, (o1[1] - o1[0]) * root)
    o3 = ((o3[1] - o3[0]) * root, (-o3[0] - o3[1]) * root)
    odd = [odd[0], o1, o2, o3]
    return [cadd(e, o) for e, o in zip(even, odd)] + [csub(e, o) for e, o in zip(even, odd)]


def fft_kernel(x_ref, m_ref, cos_ref, sin_ref, out_ref, mid):
    rows, points = x_ref.shape[2:]
    inner = points // RADIX
    chunk = 16

    @pl.loop(0, rows // chunk)
    def _(step):
        at = pl.ds(pl.multiple_of(step * chunk, chunk), chunk)
        low = pl.ds(pl.multiple_of(rows + step * chunk, chunk), chunk)
        for lane in range(0, inner, 128):
            parts = []
            for n1 in range(RADIX):
                cut = pl.ds(n1 * inner + lane, 128)
                parts.append(
                    (x_ref[0, 0, at, cut].astype(jnp.float32), x_ref[1, 0, at, cut].astype(jnp.float32))
                )
            for k1, (re, im) in enumerate(radix8(parts)):
                if k1:
                    c, s = cos_ref[k1:k1 + 1, lane:lane + 128], sin_ref[k1:k1 + 1, lane:lane + 128]
                    re, im = re * c + im * s, im * c - re * s
                re, im = re.astype(jnp.bfloat16), im.astype(jnp.bfloat16)
                left, right = pl.ds(lane, 128), pl.ds(inner + lane, 128)
                mid[k1, at, left] = re
                mid[k1, at, right] = im
                mid[k1, low, left] = im
                mid[k1, low, right] = -re

    width = 2 * rows
    for k1 in range(0, RADIX, 2):
        pair = mid[k1:k1 + 2].reshape(2 * width, 2 * inner)
        done = lax.dot_general(
            m_ref[...], pair, (((1,), (1,)), ((), ())), preferred_element_type=jnp.float32
        ).astype(jnp.bfloat16)
        for half in range(2):
            out_ref[:, :, 0, k1 + half] = done[:, half * width:(half + 1) * width].reshape(
                out_ref.shape[0], out_ref.shape[1], out_ref.shape[4], width
            )


def spectra_blocks(voltages, stat_count, local_vch):
    _, rows, items, points = voltages.shape
    inner = points // RADIX
    fine = AVG // RADIX
    matrix, cos_turn, sin_turn = dft_tables(points)
    whole = lambda shape: pl.BlockSpec(shape, lambda s: (0,) * len(shape))
    return pl.pallas_call(
        fft_kernel,
        grid=(items,),
        in_specs=[
            pl.BlockSpec((2, 1, rows, points), lambda s: (0, s, 0, 0)),
            whole(matrix.shape),
            whole(cos_turn.shape),
            whole(sin_turn.shape),
        ],
        out_specs=pl.BlockSpec(
            (stat_count, local_vch, 1, RADIX, fine, 2 * rows), lambda s: (0, 0, s, 0, 0, 0)
        ),
        out_shape=jax.ShapeDtypeStruct(
            (stat_count, local_vch, items, RADIX, fine, 2 * rows), jnp.bfloat16
        ),
        scratch_shapes=[pltpu.VMEM((RADIX, 2 * rows, 2 * inner), jnp.bfloat16)],
        name="fft",
    )(voltages.transpose(0, 2, 1, 3), matrix, cos_turn, sin_turn)


def exchange_kernel(stat_count, time_count, spec_ref, w_ref, y_ref, wg_ref, own, wown, loc, wloc,
                    send, recv, wsend, wrecv, fsend, frecv):
    me, now = lax.axis_index("stat"), lax.axis_index("tm")
    width = spec_ref.shape[-1]

    def place(time, source):
        return y_ref.at[:, time, :, pl.ds(pl.multiple_of(source * width, width), width)]

    def forward(source, src, k):
        made = []
        for j in range(1, time_count):
            copy = pltpu.make_async_remote_copy(
                src_ref=src, dst_ref=place(now, source),
                send_sem=fsend.at[j, k], recv_sem=frecv.at[j, k],
                device_id={"tm": lax.rem(now + j, time_count)}, device_id_type=pl.DeviceIdType.MESH)
            copy.start()
            made.append(copy)
        return made

    barrier = pltpu.get_barrier_semaphore()
    for k in range(1, stat_count):
        pl.semaphore_signal(barrier, inc=1, device_id={"stat": lax.rem(me + k, stat_count)},
                            device_id_type=pl.DeviceIdType.MESH)
    for j in range(1, time_count):
        pl.semaphore_signal(barrier, inc=1, device_id={"tm": lax.rem(now + j, time_count)},
                            device_id_type=pl.DeviceIdType.MESH)
    pl.semaphore_wait(barrier, stat_count + time_count - 2)

    order = sorted(range(1, stat_count), key=lambda k: (-min(k, stat_count - k), k))
    copies, wcopies = {}, {}
    for k in order:
        there = lax.rem(me + k, stat_count)
        copies[k] = pltpu.make_async_remote_copy(
            src_ref=spec_ref.at[there], dst_ref=place(now, me),
            send_sem=send.at[k], recv_sem=recv.at[k],
            device_id={"stat": there}, device_id_type=pl.DeviceIdType.MESH)
        copies[k].start()
    made = forward(me, spec_ref.at[me], 0)
    take = pltpu.make_async_copy(spec_ref.at[me], own, loc)
    wtake = pltpu.make_async_copy(w_ref, wown, wloc)
    take.start()
    wtake.start()
    for k in order:
        there = lax.rem(me + k, stat_count)
        wcopies[k] = pltpu.make_async_remote_copy(
            src_ref=w_ref, dst_ref=wg_ref.at[me],
            send_sem=wsend.at[k], recv_sem=wrecv.at[k],
            device_id={"stat": there}, device_id_type=pl.DeviceIdType.MESH)
        wcopies[k].start()
    take.wait()
    wtake.wait()
    put = pltpu.make_async_copy(own, place(now, me), loc)
    wput = pltpu.make_async_copy(wown, wg_ref.at[me], wloc)
    put.start()
    wput.start()
    for k in reversed(order):
        copies[k].wait_recv()
        source = lax.rem(me + stat_count - k, stat_count)
        made += forward(source, place(now, source), k)
    for k in order:
        copies[k].wait_send()
        wcopies[k].wait()
    put.wait()
    wput.wait()
    for copy in made:
        copy.wait()


def exchange(blocks, weights, stat_count, time_count):
    _, vch, depth, width = blocks.shape
    dma = pltpu.SemaphoreType.DMA
    peers = dma((stat_count,))
    return pl.pallas_call(
        functools.partial(exchange_kernel, stat_count, time_count),
        in_specs=[pl.BlockSpec(memory_space=pl.ANY)] * 2,
        out_specs=[pl.BlockSpec(memory_space=pl.ANY)] * 2,
        out_shape=[
            jax.ShapeDtypeStruct((vch, time_count, depth, stat_count * width), blocks.dtype),
            jax.ShapeDtypeStruct((stat_count,) + weights.shape, weights.dtype),
        ],
        scratch_shapes=[
            pltpu.VMEM(blocks.shape[1:], blocks.dtype), pltpu.VMEM(weights.shape, weights.dtype),
            dma, dma, peers, peers, peers, peers,
            dma((time_count, stat_count)), dma((time_count, stat_count)),
        ],
        compiler_params=pltpu.CompilerParams(collective_id=0, has_side_effects=True),
        name="exchange",
    )(blocks, weights)


def correlate_kernel(scale, now_ref, y_ref, w_ref, beam_ref, vis_ref, cols, left):
    now = now_ref[0]
    _, times, depth, lanes = y_ref.shape
    total = times * depth
    half = 64
    inputs = lanes // 2
    mine = vis_ref.shape[2]
    for time in range(times):
        for tile in range(0, lanes, 256):
            a = y_ref[0, time, :, tile:tile + 128]
            b = y_ref[0, time, :, tile + 128:tile + 256]
            out = pl.ds(tile // 2, 128)
            cols[pl.ds(time * depth, depth), out] = jnp.concatenate([a[:, :half], b[:, :half]], 1)
            cols[pl.ds(total + time * depth, depth), out] = jnp.concatenate([a[:, half:], b[:, half:]], 1)
    for tile in range(0, mine, 128):
        at = pl.ds(pl.multiple_of(now * mine + tile, 128), 128)
        re = (cols[pl.ds(0, total), at]).T
        im = (cols[pl.ds(total, total), at]).T
        left[pl.ds(tile, 128), pl.ds(0, total)] = re
        left[pl.ds(tile, 128), pl.ds(total, total)] = im
        left[pl.ds(mine + tile, 128), pl.ds(0, total)] = im
        left[pl.ds(mine + tile, 128), pl.ds(total, total)] = -re
    block = 256

    @pl.loop(0, inputs // block)
    def _(n):
        at = pl.ds(pl.multiple_of(n * block, block), block)
        for q in range(2):
            vis_ref[0, q, :, at] = scale * jnp.dot(
                left[pl.ds(q * mine, mine), :], cols[:, at], preferred_element_type=jnp.float32)

    beam_ref[0] = jnp.dot(
        y_ref[0, now], w_ref[...], preferred_element_type=jnp.float32).astype(jnp.bfloat16)


def correlate(spread, weights, now, scale, mine):
    vch, times, depth, lanes = spread.shape
    wide = weights.shape[1]
    inputs = lanes // 2
    return pl.pallas_call(
        functools.partial(correlate_kernel, scale),
        grid_spec=pltpu.PrefetchScalarGridSpec(
            num_scalar_prefetch=1,
            grid=(vch,),
            in_specs=[
                pl.BlockSpec((1, times, depth, lanes), lambda v, t: (v, 0, 0, 0)),
                pl.BlockSpec(weights.shape, lambda v, t: (0, 0)),
            ],
            out_specs=[
                pl.BlockSpec((1, depth, wide), lambda v, t: (v, 0, 0)),
                pl.BlockSpec((1, 2, mine, inputs), lambda v, t: (v, 0, 0, 0)),
            ],
            scratch_shapes=[
                pltpu.VMEM((2 * times * depth, inputs), jnp.bfloat16),
                pltpu.VMEM((2 * mine, 2 * times * depth), jnp.bfloat16),
            ],
        ),
        out_shape=[
            jax.ShapeDtypeStruct((vch, depth, wide), jnp.bfloat16),
            jax.ShapeDtypeStruct((vch, 2, mine, inputs), jnp.float32),
        ],
        name="correlate",
    )(now, spread, weights)


def fast_body(voltages, beam_weights):
    stat_count = lax.axis_size("stat")
    time_count = lax.axis_size("tm")
    _, rows, items, points = voltages.shape
    beams_count = beam_weights.shape[2]
    local_vch = points // stat_count // AVG
    fine = AVG // RADIX
    width = 2 * rows
    blocks = spectra_blocks(voltages, stat_count, local_vch)
    blocks = blocks.reshape(stat_count, local_vch, items * AVG, width)
    spread, gathered = exchange(blocks, beam_weights.reshape(width, beams_count), stat_count, time_count)
    gathered = gathered.reshape(stat_count, 2, rows, beams_count)
    w0, w1 = gathered[:, 0], gathered[:, 1]
    stacked = jnp.stack([jnp.concatenate([w0, w1], 2), jnp.concatenate([-w1, w0], 2)], 1)
    stacked = stacked.reshape(stat_count * width, 2 * beams_count)
    now = lax.axis_index("tm").astype(jnp.int32).reshape(1)
    scale = 1.0 / (items * time_count * AVG)
    beams, vis = correlate(spread, stacked, now, scale, stat_count * rows // time_count)
    beams = beams.reshape(local_vch, items, RADIX, fine, 2, beams_count).transpose(0, 3, 2, 1, 4, 5)
    beams = beams.reshape(local_vch * AVG, items, 2, beams_count)
    return beams, vis.transpose(2, 0, 1, 3)


def fits_tiles(mesh, voltages):
    _, inputs, spectra, points = voltages.shape
    rows = inputs // mesh.shape["stat"]
    mine = inputs // mesh.shape["tm"]
    share = points // mesh.shape["stat"]
    return 2 * rows == 128 and mine % 128 == 0 and share % AVG == 0 and spectra // mesh.shape["tm"] <= 4 and mesh.shape["tm"] <= 2


def solution(mesh):
    def whole(voltages, beam_weights):
        return jax.shard_map(
            fast_body if fits_tiles(mesh, voltages) else body,
            mesh=mesh,
            in_specs=(P(None, "stat", "tm", None), P(None, "stat", None)),
            out_specs=(P("stat", "tm", None, None), P("tm", "stat", None, None)),
            check_vma=False,
        )(voltages, beam_weights)

    return whole
```

```python
import functools
import math

import jax
import jax.numpy as jnp
import numpy as np
from jax import lax
from jax.experimental import pallas as pl
from jax.experimental.pallas import tpu as pltpu
from jax.sharding import PartitionSpec as P

NA = 16
NB = 256
AVG = 128


def dft_block(length):
    index = jnp.arange(length, dtype=jnp.int32)
    product = index[:, None] * index[None, :] % length
    angle = product.astype(jnp.float32) * (2.0 * math.pi / length)
    cosine = jnp.cos(angle)
    sine = jnp.sin(angle)
    return jnp.stack([jnp.stack([cosine, -sine]), jnp.stack([sine, cosine])])


def fine_spectra(voltages):
    block_inputs = voltages.shape[1]
    spectra_count = voltages.shape[2]
    signal = voltages.astype(jnp.float32).reshape(2, block_inputs, spectra_count, NA, NB)
    first = jnp.einsum("poak,pisab->osikb", dft_block(NA), signal, precision=lax.Precision.HIGH)
    outer_index = jnp.arange(NA, dtype=jnp.int32)
    inner_index = jnp.arange(NB, dtype=jnp.int32)
    rotation = (outer_index[:, None] * inner_index[None, :] % (NA * NB)).astype(jnp.float32) * (
        2.0 * math.pi / (NA * NB)
    )
    cos_twist = jnp.cos(rotation)
    sin_twist = jnp.sin(rotation)
    rotated = jnp.stack(
        [first[0] * cos_twist + first[1] * sin_twist, first[1] * cos_twist - first[0] * sin_twist]
    )
    final = jnp.einsum("osikb,ocbq->csiqk", rotated, dft_block(NB), precision=lax.Precision.HIGH)
    norm_factor = 1.0 / math.sqrt(NA * NB)
    return (
        (final * norm_factor).reshape(2, spectra_count, block_inputs, NA * NB).astype(jnp.bfloat16)
    )


def stack_weights(weights):
    return jnp.stack(
        [jnp.stack([weights[0], weights[1]], 1), jnp.stack([-weights[1], weights[0]], 1)], 0
    )


def body(voltages, beam_weights):
    stat_count = lax.axis_size("stat")
    time_count = lax.axis_size("tm")
    block_inputs = voltages.shape[1]
    spectra = fine_spectra(voltages)
    spectra_count = spectra.shape[1]
    channel_share = NA * NB // stat_count
    all_weights = lax.all_gather(beam_weights, "stat", axis=1, tiled=True)
    full_stack = stack_weights(all_weights)
    turned = lax.all_to_all(spectra, "stat", split_axis=3, concat_axis=2, tiled=True)
    item_count = turned.shape[1]

    def add_block(block_index, running):
        offset = (block_index * block_inputs).astype(jnp.int32)
        spec_block = lax.dynamic_slice_in_dim(turned, offset, block_inputs, 2)
        weight_block = lax.dynamic_slice_in_dim(full_stack, offset, block_inputs, 1)
        partial_value = jnp.einsum(
            "psic,piqb->csqb", spec_block, weight_block, preferred_element_type=jnp.float32
        )
        rounded = lax.optimization_barrier(partial_value.astype(jnp.bfloat16))
        return running + rounded.astype(jnp.float32)

    initial = jnp.zeros((turned.shape[3], item_count, 2, beam_weights.shape[2]), jnp.float32)
    beams = lax.fori_loop(0, stat_count, add_block, initial).astype(jnp.bfloat16)
    local_vch = channel_share // AVG
    scale = 1.0 / (spectra_count * time_count * AVG)
    split = turned.reshape(2, spectra_count, stat_count * block_inputs, local_vch, AVG)
    real_gram = jnp.einsum("psiva,psjva->ivj", split, split, preferred_element_type=jnp.float32)
    mixed = jnp.einsum("siva,sjva->ivj", split[1], split[0], preferred_element_type=jnp.float32)
    mixed = mixed - jnp.einsum(
        "siva,sjva->ivj", split[0], split[1], preferred_element_type=jnp.float32
    )
    visibilities = lax.psum_scatter(
        (jnp.stack([real_gram, mixed], axis=2) * scale).astype(jnp.bfloat16),
        "tm",
        scatter_dimension=0,
        tiled=True,
    ).astype(jnp.float32)
    return (beams, visibilities)

RADIX = 8


def dft_tables(points):
    inner = points // RADIX
    index = np.arange(inner)
    angle = 2.0 * np.pi * (index[:, None] * index[None, :] % inner) / inner
    scale = 1.0 / math.sqrt(points)
    matrix = np.concatenate([np.cos(angle), np.sin(angle)], 1) * scale
    turn = 2.0 * np.pi * (np.arange(RADIX)[:, None] * index[None, :]) / points
    return (
        jnp.asarray(matrix, jnp.bfloat16),
        jnp.asarray(np.cos(turn), jnp.float32),
        jnp.asarray(np.sin(turn), jnp.float32),
    )


def cadd(a, b):
    return a[0] + b[0], a[1] + b[1]


def csub(a, b):
    return a[0] - b[0], a[1] - b[1]


def times_minus_i(a):
    return a[1], -a[0]


def radix4(a):
    s02, d02 = cadd(a[0], a[2]), csub(a[0], a[2])
    s13, d13 = cadd(a[1], a[3]), times_minus_i(csub(a[1], a[3]))
    return [cadd(s02, s13), cadd(d02, d13), csub(s02, s13), csub(d02, d13)]


def radix8(a):
    even, odd = radix4(a[0::2]), radix4(a[1::2])
    root = math.sqrt(0.5)
    o1, o2, o3 = odd[1], times_minus_i(odd[2]), odd[3]
    o1 = ((o1[0] + o1[1]) * root, (o1[1] - o1[0]) * root)
    o3 = ((o3[1] - o3[0]) * root, (-o3[0] - o3[1]) * root)
    odd = [odd[0], o1, o2, o3]
    return [cadd(e, o) for e, o in zip(even, odd)] + [csub(e, o) for e, o in zip(even, odd)]


def fft_kernel(x_ref, m_ref, cos_ref, sin_ref, out_ref, mid):
    rows, points = x_ref.shape[2:]
    inner = points // RADIX
    chunk = 16

    @pl.loop(0, rows // chunk)
    def _(step):
        at = pl.ds(pl.multiple_of(step * chunk, chunk), chunk)
        low = pl.ds(pl.multiple_of(rows + step * chunk, chunk), chunk)
        for lane in range(0, inner, 128):
            parts = []
            for n1 in range(RADIX):
                cut = pl.ds(n1 * inner + lane, 128)
                parts.append(
                    (x_ref[0, 0, at, cut].astype(jnp.float32), x_ref[1, 0, at, cut].astype(jnp.float32))
                )
            for k1, (re, im) in enumerate(radix8(parts)):
                if k1:
                    c, s = cos_ref[k1:k1 + 1, lane:lane + 128], sin_ref[k1:k1 + 1, lane:lane + 128]
                    re, im = re * c + im * s, im * c - re * s
                re, im = re.astype(jnp.bfloat16), im.astype(jnp.bfloat16)
                left, right = pl.ds(lane, 128), pl.ds(inner + lane, 128)
                mid[k1, at, left] = re
                mid[k1, at, right] = im
                mid[k1, low, left] = im
                mid[k1, low, right] = -re

    width = 2 * rows
    for k1 in range(0, RADIX, 2):
        pair = mid[k1:k1 + 2].reshape(2 * width, 2 * inner)
        done = lax.dot_general(
            m_ref[...], pair, (((1,), (1,)), ((), ())), preferred_element_type=jnp.float32
        ).astype(jnp.bfloat16)
        for half in range(2):
            out_ref[:, :, 0, k1 + half] = done[:, half * width:(half + 1) * width].reshape(
                out_ref.shape[0], out_ref.shape[1], out_ref.shape[4], width
            )


def spectra_blocks(voltages, stat_count, local_vch):
    _, rows, items, points = voltages.shape
    inner = points // RADIX
    fine = AVG // RADIX
    matrix, cos_turn, sin_turn = dft_tables(points)
    whole = lambda shape: pl.BlockSpec(shape, lambda s: (0,) * len(shape))
    return pl.pallas_call(
        fft_kernel,
        grid=(items,),
        in_specs=[
            pl.BlockSpec((2, 1, rows, points), lambda s: (0, s, 0, 0)),
            whole(matrix.shape),
            whole(cos_turn.shape),
            whole(sin_turn.shape),
        ],
        out_specs=pl.BlockSpec(
            (stat_count, local_vch, 1, RADIX, fine, 2 * rows), lambda s: (0, 0, s, 0, 0, 0)
        ),
        out_shape=jax.ShapeDtypeStruct(
            (stat_count, local_vch, items, RADIX, fine, 2 * rows), jnp.bfloat16
        ),
        scratch_shapes=[pltpu.VMEM((RADIX, 2 * rows, 2 * inner), jnp.bfloat16)],
        name="fft",
    )(voltages.transpose(0, 2, 1, 3), matrix, cos_turn, sin_turn)


def send_order(count):
    near = []
    half = 1
    while half < count // 4:
        near += [(half, j) for j in range(half)]
        half *= 2
    far = [(count // 2, j) for j in range(count // 2)]
    middle = [(half, j) for j in range(half)] if half < count // 2 else []
    mixed = []
    while far or middle:
        mixed += far[:2] + middle[:1]
        far, middle = far[2:], middle[1:]
    return near + mixed


def exchange_kernel(stat_count, time_count, spec_ref, w_ref, y_ref, wg_ref, own, wown, loc, wloc,
                    send, recv, wsend, wrecv, fsend, frecv):
    me, now = lax.axis_index("stat"), lax.axis_index("tm")
    width = spec_ref.shape[-1]

    def place(time, source):
        return y_ref.at[:, time, :, pl.ds(pl.multiple_of(source * width, width), width)]

    def forward(source, src, k):
        made = []
        for j in range(1, time_count):
            copy = pltpu.make_async_remote_copy(
                src_ref=src, dst_ref=place(now, source),
                send_sem=fsend.at[j, k], recv_sem=frecv.at[j, k],
                device_id={"tm": lax.rem(now + j, time_count)}, device_id_type=pl.DeviceIdType.MESH)
            copy.start()
            made.append(copy)
        return made

    barrier = pltpu.get_barrier_semaphore()
    for k in range(1, stat_count):
        pl.semaphore_signal(barrier, inc=1, device_id={"stat": lax.rem(me + k, stat_count)},
                            device_id_type=pl.DeviceIdType.MESH)
    for j in range(1, time_count):
        pl.semaphore_signal(barrier, inc=1, device_id={"tm": lax.rem(now + j, time_count)},
                            device_id_type=pl.DeviceIdType.MESH)
    pl.semaphore_wait(barrier, stat_count + time_count - 2)

    order = send_order(stat_count)

    def partner(k, sign):
        half = k[0]
        other = me // half + 1 - 2 * lax.rem(me // half, 2)
        return other * half + lax.rem(lax.rem(me, half) + half + sign * k[1], half)

    copies, wcopies = {}, {}
    for slot, k in enumerate(order, 1):
        there = partner(k, 1)
        copies[k] = pltpu.make_async_remote_copy(
            src_ref=spec_ref.at[there], dst_ref=place(now, me),
            send_sem=send.at[slot], recv_sem=recv.at[slot],
            device_id={"stat": there}, device_id_type=pl.DeviceIdType.MESH)
        copies[k].start()
    made = forward(me, spec_ref.at[me], 0)
    take = pltpu.make_async_copy(spec_ref.at[me], own, loc)
    wtake = pltpu.make_async_copy(w_ref, wown, wloc)
    take.start()
    wtake.start()
    for slot, k in enumerate(order, 1):
        there = partner(k, 1)
        wcopies[k] = pltpu.make_async_remote_copy(
            src_ref=w_ref, dst_ref=wg_ref.at[me],
            send_sem=wsend.at[slot], recv_sem=wrecv.at[slot],
            device_id={"stat": there}, device_id_type=pl.DeviceIdType.MESH)
        wcopies[k].start()
    take.wait()
    wtake.wait()
    put = pltpu.make_async_copy(own, place(now, me), loc)
    wput = pltpu.make_async_copy(wown, wg_ref.at[me], wloc)
    put.start()
    wput.start()
    for slot, k in enumerate(order, 1):
        copies[k].wait_recv()
        source = partner(k, -1)
        made += forward(source, place(now, source), slot)
    for k in order:
        copies[k].wait_send()
        wcopies[k].wait()
    put.wait()
    wput.wait()
    for copy in made:
        copy.wait()


def exchange(blocks, weights, stat_count, time_count):
    _, vch, depth, width = blocks.shape
    dma = pltpu.SemaphoreType.DMA
    peers = dma((stat_count,))
    return pl.pallas_call(
        functools.partial(exchange_kernel, stat_count, time_count),
        in_specs=[pl.BlockSpec(memory_space=pl.ANY)] * 2,
        out_specs=[pl.BlockSpec(memory_space=pl.ANY)] * 2,
        out_shape=[
            jax.ShapeDtypeStruct((vch, time_count, depth, stat_count * width), blocks.dtype),
            jax.ShapeDtypeStruct((stat_count,) + weights.shape, weights.dtype),
        ],
        scratch_shapes=[
            pltpu.VMEM(blocks.shape[1:], blocks.dtype), pltpu.VMEM(weights.shape, weights.dtype),
            dma, dma, peers, peers, peers, peers,
            dma((time_count, stat_count)), dma((time_count, stat_count)),
        ],
        compiler_params=pltpu.CompilerParams(collective_id=0, has_side_effects=True),
        name="exchange",
    )(blocks, weights)


def correlate_kernel(scale, now_ref, y_ref, w_ref, beam_ref, vis_ref, cols, left, stacked):
    now = now_ref[0]
    _, times, depth, lanes = y_ref.shape
    total = times * depth
    half = 64
    inputs = lanes // 2
    mine = vis_ref.shape[0]
    groups = vis_ref.shape[2]
    flat = vis_ref.reshape(mine * groups, 128)
    width, beams = w_ref.shape[1:]
    rows = width // 2
    for time in range(times):
        for tile in range(0, lanes, 256):
            a = y_ref[0, time, :, tile:tile + 128]
            b = y_ref[0, time, :, tile + 128:tile + 256]
            out = pl.ds(tile // 2, 128)
            cols[pl.ds(time * depth, depth), out] = jnp.concatenate([a[:, :half], b[:, :half]], 1)
            cols[pl.ds(total + time * depth, depth), out] = jnp.concatenate([a[:, half:], b[:, half:]], 1)
    for tile in range(0, mine, 128):
        at = pl.ds(pl.multiple_of(now * mine + tile, 128), 128)
        re = (cols[pl.ds(0, total), at]).T
        im = (cols[pl.ds(total, total), at]).T
        left[pl.ds(tile, 128), pl.ds(0, total)] = re
        left[pl.ds(tile, 128), pl.ds(total, total)] = im
        left[pl.ds(mine + tile, 128), pl.ds(0, total)] = im
        left[pl.ds(mine + tile, 128), pl.ds(total, total)] = -re
    block = 256

    @pl.loop(0, inputs // block)
    def _(n):
        at = pl.ds(pl.multiple_of(n * block, block), block)
        for q in range(2):
            value = scale * jnp.dot(
                left[pl.ds(q * mine, mine), :], cols[:, at], preferred_element_type=jnp.float32)
            for part in range(block // 128):
                row = (n * (block // 128) + part) * 2 + q
                flat[pl.ds(row, mine, stride=groups), :] = value[:, part * 128:part * 128 + 128]

    for source in range(w_ref.shape[0]):
        upper = pl.ds(source * width, rows)
        lower = pl.ds(source * width + rows, rows)
        stacked[upper, pl.ds(0, beams)] = w_ref[source, :rows]
        stacked[upper, pl.ds(beams, beams)] = w_ref[source, rows:]
        stacked[lower, pl.ds(0, beams)] = -w_ref[source, rows:]
        stacked[lower, pl.ds(beams, beams)] = w_ref[source, :rows]
    beam_ref[0] = jnp.dot(
        y_ref[0, now], stacked[...], preferred_element_type=jnp.float32).astype(jnp.bfloat16)


def correlate(spread, weights, now, scale, mine):
    vch, times, depth, lanes = spread.shape
    wide = 2 * weights.shape[2]
    groups = lanes // 128
    inputs = lanes // 2
    return pl.pallas_call(
        functools.partial(correlate_kernel, scale),
        grid_spec=pltpu.PrefetchScalarGridSpec(
            num_scalar_prefetch=1,
            grid=(vch,),
            in_specs=[
                pl.BlockSpec((1, times, depth, lanes), lambda v, t: (v, 0, 0, 0)),
                pl.BlockSpec(weights.shape, lambda v, t: (0, 0, 0)),
            ],
            out_specs=[
                pl.BlockSpec((1, depth, wide), lambda v, t: (v, 0, 0)),
                pl.BlockSpec((mine, 1, groups, 128), lambda v, t: (0, v, 0, 0)),
            ],
            scratch_shapes=[
                pltpu.VMEM((2 * times * depth, inputs), jnp.bfloat16),
                pltpu.VMEM((2 * mine, 2 * times * depth), jnp.bfloat16),
                pltpu.VMEM((lanes, wide), jnp.bfloat16),
            ],
        ),
        out_shape=[
            jax.ShapeDtypeStruct((vch, depth, wide), jnp.bfloat16),
            jax.ShapeDtypeStruct((mine, vch, groups, 128), jnp.float32),
        ],
        name="correlate",
    )(now, spread, weights)


def fast_body(voltages, beam_weights):
    stat_count = lax.axis_size("stat")
    time_count = lax.axis_size("tm")
    _, rows, items, points = voltages.shape
    beams_count = beam_weights.shape[2]
    local_vch = points // stat_count // AVG
    fine = AVG // RADIX
    width = 2 * rows
    blocks = spectra_blocks(voltages, stat_count, local_vch)
    blocks = blocks.reshape(stat_count, local_vch, items * AVG, width)
    spread, gathered = exchange(blocks, beam_weights.reshape(width, beams_count), stat_count, time_count)
    now = lax.axis_index("tm").astype(jnp.int32).reshape(1)
    scale = 1.0 / (items * time_count * AVG)
    beams, vis = correlate(spread, gathered, now, scale, stat_count * rows // time_count)
    beams = beams.reshape(local_vch, items, RADIX, fine, 2, beams_count).transpose(0, 3, 2, 1, 4, 5)
    beams = beams.reshape(local_vch * AVG, items, 2, beams_count)
    vis = vis.reshape(vis.shape[0], local_vch, -1, 2, 128).transpose(0, 1, 3, 2, 4)
    return beams, vis.reshape(vis.shape[0], local_vch, 2, stat_count * rows)


def fits_tiles(mesh, voltages):
    _, inputs, spectra, points = voltages.shape
    rows = inputs // mesh.shape["stat"]
    mine = inputs // mesh.shape["tm"]
    share = points // mesh.shape["stat"]
    even = mesh.shape["stat"] & (mesh.shape["stat"] - 1) == 0 and mesh.shape["stat"] >= 4
    return even and 2 * rows == 128 and mine % 128 == 0 and share % AVG == 0 and spectra // mesh.shape["tm"] <= 4 and mesh.shape["tm"] <= 2


def solution(mesh):
    def whole(voltages, beam_weights):
        return jax.shard_map(
            fast_body if fits_tiles(mesh, voltages) else body,
            mesh=mesh,
            in_specs=(P(None, "stat", "tm", None), P(None, "stat", None)),
            out_specs=(P("stat", "tm", None, None), P("tm", "stat", None, None)),
            check_vma=False,
        )(voltages, beam_weights)

    return whole
```

```python
import functools
import math

import jax
import jax.numpy as jnp
import numpy as np
from jax import lax
from jax.experimental import pallas as pl
from jax.experimental.pallas import tpu as pltpu
from jax.sharding import PartitionSpec as P

NA = 16
NB = 256
AVG = 128


def dft_block(length):
    index = jnp.arange(length, dtype=jnp.int32)
    product = index[:, None] * index[None, :] % length
    angle = product.astype(jnp.float32) * (2.0 * math.pi / length)
    cosine = jnp.cos(angle)
    sine = jnp.sin(angle)
    return jnp.stack([jnp.stack([cosine, -sine]), jnp.stack([sine, cosine])])


def fine_spectra(voltages):
    block_inputs = voltages.shape[1]
    spectra_count = voltages.shape[2]
    signal = voltages.astype(jnp.float32).reshape(2, block_inputs, spectra_count, NA, NB)
    first = jnp.einsum("poak,pisab->osikb", dft_block(NA), signal, precision=lax.Precision.HIGH)
    outer_index = jnp.arange(NA, dtype=jnp.int32)
    inner_index = jnp.arange(NB, dtype=jnp.int32)
    rotation = (outer_index[:, None] * inner_index[None, :] % (NA * NB)).astype(jnp.float32) * (
        2.0 * math.pi / (NA * NB)
    )
    cos_twist = jnp.cos(rotation)
    sin_twist = jnp.sin(rotation)
    rotated = jnp.stack(
        [first[0] * cos_twist + first[1] * sin_twist, first[1] * cos_twist - first[0] * sin_twist]
    )
    final = jnp.einsum("osikb,ocbq->csiqk", rotated, dft_block(NB), precision=lax.Precision.HIGH)
    norm_factor = 1.0 / math.sqrt(NA * NB)
    return (
        (final * norm_factor).reshape(2, spectra_count, block_inputs, NA * NB).astype(jnp.bfloat16)
    )


def stack_weights(weights):
    return jnp.stack(
        [jnp.stack([weights[0], weights[1]], 1), jnp.stack([-weights[1], weights[0]], 1)], 0
    )


def body(voltages, beam_weights):
    stat_count = lax.axis_size("stat")
    time_count = lax.axis_size("tm")
    block_inputs = voltages.shape[1]
    spectra = fine_spectra(voltages)
    spectra_count = spectra.shape[1]
    channel_share = NA * NB // stat_count
    all_weights = lax.all_gather(beam_weights, "stat", axis=1, tiled=True)
    full_stack = stack_weights(all_weights)
    turned = lax.all_to_all(spectra, "stat", split_axis=3, concat_axis=2, tiled=True)
    item_count = turned.shape[1]

    def add_block(block_index, running):
        offset = (block_index * block_inputs).astype(jnp.int32)
        spec_block = lax.dynamic_slice_in_dim(turned, offset, block_inputs, 2)
        weight_block = lax.dynamic_slice_in_dim(full_stack, offset, block_inputs, 1)
        partial_value = jnp.einsum(
            "psic,piqb->csqb", spec_block, weight_block, preferred_element_type=jnp.float32
        )
        rounded = lax.optimization_barrier(partial_value.astype(jnp.bfloat16))
        return running + rounded.astype(jnp.float32)

    initial = jnp.zeros((turned.shape[3], item_count, 2, beam_weights.shape[2]), jnp.float32)
    beams = lax.fori_loop(0, stat_count, add_block, initial).astype(jnp.bfloat16)
    local_vch = channel_share // AVG
    scale = 1.0 / (spectra_count * time_count * AVG)
    split = turned.reshape(2, spectra_count, stat_count * block_inputs, local_vch, AVG)
    real_gram = jnp.einsum("psiva,psjva->ivj", split, split, preferred_element_type=jnp.float32)
    mixed = jnp.einsum("siva,sjva->ivj", split[1], split[0], preferred_element_type=jnp.float32)
    mixed = mixed - jnp.einsum(
        "siva,sjva->ivj", split[0], split[1], preferred_element_type=jnp.float32
    )
    visibilities = lax.psum_scatter(
        (jnp.stack([real_gram, mixed], axis=2) * scale).astype(jnp.bfloat16),
        "tm",
        scatter_dimension=0,
        tiled=True,
    ).astype(jnp.float32)
    return (beams, visibilities)

RADIX = 8


def dft_tables(points):
    inner = points // RADIX
    index = np.arange(inner)
    angle = 2.0 * np.pi * (index[:, None] * index[None, :] % inner) / inner
    scale = 1.0 / math.sqrt(points)
    matrix = np.concatenate([np.cos(angle), np.sin(angle)], 1) * scale
    turn = 2.0 * np.pi * (np.arange(RADIX)[:, None] * index[None, :]) / points
    return (
        jnp.asarray(matrix, jnp.bfloat16),
        jnp.asarray(np.cos(turn), jnp.float32),
        jnp.asarray(np.sin(turn), jnp.float32),
    )


def cadd(a, b):
    return a[0] + b[0], a[1] + b[1]


def csub(a, b):
    return a[0] - b[0], a[1] - b[1]


def times_minus_i(a):
    return a[1], -a[0]


def radix4(a):
    s02, d02 = cadd(a[0], a[2]), csub(a[0], a[2])
    s13, d13 = cadd(a[1], a[3]), times_minus_i(csub(a[1], a[3]))
    return [cadd(s02, s13), cadd(d02, d13), csub(s02, s13), csub(d02, d13)]


def radix8(a):
    even, odd = radix4(a[0::2]), radix4(a[1::2])
    root = math.sqrt(0.5)
    o1, o2, o3 = odd[1], times_minus_i(odd[2]), odd[3]
    o1 = ((o1[0] + o1[1]) * root, (o1[1] - o1[0]) * root)
    o3 = ((o3[1] - o3[0]) * root, (-o3[0] - o3[1]) * root)
    odd = [odd[0], o1, o2, o3]
    return [cadd(e, o) for e, o in zip(even, odd)] + [csub(e, o) for e, o in zip(even, odd)]


def fft_kernel(x_ref, m_ref, cos_ref, sin_ref, out_ref, mid):
    rows, points = x_ref.shape[2:]
    inner = points // RADIX
    chunk = 16

    @pl.loop(0, rows // chunk)
    def _(step):
        at = pl.ds(pl.multiple_of(step * chunk, chunk), chunk)
        low = pl.ds(pl.multiple_of(rows + step * chunk, chunk), chunk)
        for lane in range(0, inner, 128):
            parts = []
            for n1 in range(RADIX):
                cut = pl.ds(n1 * inner + lane, 128)
                parts.append(
                    (x_ref[0, 0, at, cut].astype(jnp.float32), x_ref[1, 0, at, cut].astype(jnp.float32))
                )
            for k1, (re, im) in enumerate(radix8(parts)):
                if k1:
                    c, s = cos_ref[k1:k1 + 1, lane:lane + 128], sin_ref[k1:k1 + 1, lane:lane + 128]
                    re, im = re * c + im * s, im * c - re * s
                re, im = re.astype(jnp.bfloat16), im.astype(jnp.bfloat16)
                left, right = pl.ds(lane, 128), pl.ds(inner + lane, 128)
                mid[k1, at, left] = re
                mid[k1, at, right] = im
                mid[k1, low, left] = im
                mid[k1, low, right] = -re

    width = 2 * rows
    for k1 in range(0, RADIX, 2):
        pair = mid[k1:k1 + 2].reshape(2 * width, 2 * inner)
        done = lax.dot_general(
            m_ref[...], pair, (((1,), (1,)), ((), ())), preferred_element_type=jnp.float32
        ).astype(jnp.bfloat16)
        for half in range(2):
            out_ref[:, :, 0, k1 + half] = done[:, half * width:(half + 1) * width].reshape(
                out_ref.shape[0], out_ref.shape[1], out_ref.shape[4], width
            )


def spectra_blocks(voltages, stat_count, local_vch):
    _, rows, items, points = voltages.shape
    inner = points // RADIX
    fine = AVG // RADIX
    matrix, cos_turn, sin_turn = dft_tables(points)
    whole = lambda shape: pl.BlockSpec(shape, lambda s: (0,) * len(shape))
    return pl.pallas_call(
        fft_kernel,
        grid=(items,),
        in_specs=[
            pl.BlockSpec((2, 1, rows, points), lambda s: (0, s, 0, 0)),
            whole(matrix.shape),
            whole(cos_turn.shape),
            whole(sin_turn.shape),
        ],
        out_specs=pl.BlockSpec(
            (stat_count, local_vch, 1, RADIX, fine, 2 * rows), lambda s: (0, 0, s, 0, 0, 0)
        ),
        out_shape=jax.ShapeDtypeStruct(
            (stat_count, local_vch, items, RADIX, fine, 2 * rows), jnp.bfloat16
        ),
        scratch_shapes=[pltpu.VMEM((RADIX, 2 * rows, 2 * inner), jnp.bfloat16)],
        name="fft",
    )(voltages.transpose(0, 2, 1, 3), matrix, cos_turn, sin_turn)


def exchange_kernel(stat_count, time_count, spec_ref, w_ref, y_ref, wg_ref, own, wown, loc, wloc,
                    send, recv, wsend, wrecv, fsend, frecv):
    me, now = lax.axis_index("stat"), lax.axis_index("tm")

    def place(time, source):
        return y_ref.at[time, source]

    def forward(source, src, k):
        made = []
        for j in range(1, time_count):
            copy = pltpu.make_async_remote_copy(
                src_ref=src, dst_ref=place(now, source),
                send_sem=fsend.at[j, k], recv_sem=frecv.at[j, k],
                device_id={"tm": lax.rem(now + j, time_count)}, device_id_type=pl.DeviceIdType.MESH)
            copy.start()
            made.append(copy)
        return made

    barrier = pltpu.get_barrier_semaphore()
    for k in range(1, stat_count):
        pl.semaphore_signal(barrier, inc=1, device_id={"stat": lax.rem(me + k, stat_count)},
                            device_id_type=pl.DeviceIdType.MESH)
    for j in range(1, time_count):
        pl.semaphore_signal(barrier, inc=1, device_id={"tm": lax.rem(now + j, time_count)},
                            device_id_type=pl.DeviceIdType.MESH)
    pl.semaphore_wait(barrier, stat_count + time_count - 2)

    half, quarter = stat_count // 2, stat_count // 4
    upper = me // half
    spot = lax.rem(me, quarter)
    inner = lax.rem(me // quarter + upper, 2)

    def turned(base, sign, r):
        return base + lax.rem(spot + quarter + sign * r, quarter)

    bases = ((1 - upper) * half + upper * quarter, (1 - upper) * (half + quarter))
    beside = (2 * upper + 1 - lax.rem(me // quarter, 2)) * quarter
    own_quarter = me // quarter * quarter
    sends, sources = [], []
    for r in range(1, quarter):
        sends.append((turned(own_quarter, 1, r), r))
        sources.append((turned(own_quarter, -1, r), r))
    for r in range(quarter):
        for place_of in range(2):
            sends.append((turned(bases[place_of], 1, r), 2 * quarter + (1 - inner) * quarter + r))
        sends.append((turned(beside, 1, r), quarter + r))
        sources.append((turned(beside, -1, r), quarter + r))
        sources.append((turned(bases[0], -1, r), 2 * quarter + r))
    for r in range(quarter):
        sources.append((turned(bases[1], -1, r), 3 * quarter + r))

    def to(src, dst, there, out_sem, in_sem):
        return pltpu.make_async_remote_copy(
            src_ref=src, dst_ref=dst, send_sem=out_sem, recv_sem=in_sem,
            device_id={"stat": there}, device_id_type=pl.DeviceIdType.MESH)

    copies, wcopies = [], []
    for number, (there, slot) in enumerate(sends):
        copies.append(to(spec_ref.at[there], place(now, me), there, send.at[number], recv.at[slot]))
        copies[-1].start()
    made = forward(me, spec_ref.at[me], 0)
    take = pltpu.make_async_copy(spec_ref.at[me], own, loc)
    wtake = pltpu.make_async_copy(w_ref, wown, wloc)
    take.start()
    wtake.start()
    for number, (there, slot) in enumerate(sends):
        wcopies.append(to(w_ref, wg_ref.at[me], there, wsend.at[number], wrecv.at[slot]))
        wcopies[-1].start()
    take.wait()
    wtake.wait()
    put = pltpu.make_async_copy(own, place(now, me), loc)
    wput = pltpu.make_async_copy(wown, wg_ref.at[me], wloc)
    put.start()
    wput.start()
    for source, slot in sources:
        to(spec_ref.at[source], place(now, source), source, send.at[0], recv.at[slot]).wait_recv()
        made += forward(source, place(now, source), slot)
    for source, slot in sources:
        to(w_ref, wg_ref.at[source], source, wsend.at[0], wrecv.at[slot]).wait_recv()
    for copy in copies + wcopies:
        copy.wait_send()
    put.wait()
    wput.wait()
    for copy in made:
        copy.wait()


def exchange(blocks, weights, stat_count, time_count):
    dma = pltpu.SemaphoreType.DMA
    peers = dma((stat_count,))
    return pl.pallas_call(
        functools.partial(exchange_kernel, stat_count, time_count),
        in_specs=[pl.BlockSpec(memory_space=pl.ANY)] * 2,
        out_specs=[pl.BlockSpec(memory_space=pl.ANY)] * 2,
        out_shape=[
            jax.ShapeDtypeStruct((time_count,) + blocks.shape, blocks.dtype),
            jax.ShapeDtypeStruct((stat_count,) + weights.shape, weights.dtype),
        ],
        scratch_shapes=[
            pltpu.VMEM(blocks.shape[1:], blocks.dtype), pltpu.VMEM(weights.shape, weights.dtype),
            dma, dma, peers, peers, peers, peers,
            dma((time_count, stat_count)), dma((time_count, stat_count)),
        ],
        compiler_params=pltpu.CompilerParams(collective_id=0, has_side_effects=True),
        name="exchange",
    )(blocks, weights)


def correlate_kernel(scale, now_ref, y_ref, w_ref, beam_ref, vis_ref, cols, left, stacked):
    now = now_ref[0]
    times, sources, _, depth, width = y_ref.shape
    total = times * depth
    half = width // 2
    inputs = sources * half
    mine = vis_ref.shape[0]
    groups = vis_ref.shape[2]
    flat = vis_ref.reshape(mine * groups, 128)
    beams = w_ref.shape[2]
    for time in range(times):
        for source in range(0, sources, 2):
            a = y_ref[time, source, 0]
            b = y_ref[time, source + 1, 0]
            out = pl.ds(source * half, width)
            cols[pl.ds(time * depth, depth), out] = jnp.concatenate([a[:, :half], b[:, :half]], 1)
            cols[pl.ds(total + time * depth, depth), out] = jnp.concatenate([a[:, half:], b[:, half:]], 1)
    for tile in range(0, mine, 128):
        at = pl.ds(pl.multiple_of(now * mine + tile, 128), 128)
        re = (cols[pl.ds(0, total), at]).T
        im = (cols[pl.ds(total, total), at]).T
        left[pl.ds(tile, 128), pl.ds(0, total)] = re
        left[pl.ds(tile, 128), pl.ds(total, total)] = im
        left[pl.ds(mine + tile, 128), pl.ds(0, total)] = im
        left[pl.ds(mine + tile, 128), pl.ds(total, total)] = -re
    block = 256

    @pl.loop(0, inputs // block)
    def _(n):
        at = pl.ds(pl.multiple_of(n * block, block), block)
        for q in range(2):
            value = scale * jnp.dot(
                left[pl.ds(q * mine, mine), :], cols[:, at], preferred_element_type=jnp.float32)
            for part in range(block // 128):
                row = (n * (block // 128) + part) * 2 + q
                flat[pl.ds(row, mine, stride=groups), :] = value[:, part * 128:part * 128 + 128]

    for source in range(sources):
        upper = pl.ds(source * half, half)
        lower = pl.ds(inputs + source * half, half)
        stacked[upper, pl.ds(0, beams)] = w_ref[source, :half]
        stacked[upper, pl.ds(beams, beams)] = w_ref[source, half:]
        stacked[lower, pl.ds(0, beams)] = -w_ref[source, half:]
        stacked[lower, pl.ds(beams, beams)] = w_ref[source, :half]
    shift = pl.multiple_of(now * depth, depth)
    real = jnp.dot(
        cols[pl.ds(shift, depth), :], stacked[pl.ds(0, inputs), :], preferred_element_type=jnp.float32)
    imag = jnp.dot(
        cols[pl.ds(total + shift, depth), :], stacked[pl.ds(inputs, inputs), :],
        preferred_element_type=jnp.float32)
    beam_ref[0] = (real + imag).astype(jnp.bfloat16)


def correlate(spread, weights, now, scale, mine):
    times, sources, vch, depth, width = spread.shape
    lanes = sources * width
    wide = 2 * weights.shape[2]
    groups = lanes // 128
    inputs = lanes // 2
    return pl.pallas_call(
        functools.partial(correlate_kernel, scale),
        grid_spec=pltpu.PrefetchScalarGridSpec(
            num_scalar_prefetch=1,
            grid=(vch,),
            in_specs=[
                pl.BlockSpec((times, sources, 1, depth, width), lambda v, t: (0, 0, v, 0, 0)),
                pl.BlockSpec(weights.shape, lambda v, t: (0, 0, 0)),
            ],
            out_specs=[
                pl.BlockSpec((1, depth, wide), lambda v, t: (v, 0, 0)),
                pl.BlockSpec((mine, 1, groups, 128), lambda v, t: (0, v, 0, 0)),
            ],
            scratch_shapes=[
                pltpu.VMEM((2 * times * depth, inputs), jnp.bfloat16),
                pltpu.VMEM((2 * mine, 2 * times * depth), jnp.bfloat16),
                pltpu.VMEM((lanes, wide), jnp.bfloat16),
            ],
        ),
        out_shape=[
            jax.ShapeDtypeStruct((vch, depth, wide), jnp.bfloat16),
            jax.ShapeDtypeStruct((mine, vch, groups, 128), jnp.float32),
        ],
        name="correlate",
    )(now, spread, weights)


def fast_body(voltages, beam_weights):
    stat_count = lax.axis_size("stat")
    time_count = lax.axis_size("tm")
    _, rows, items, points = voltages.shape
    beams_count = beam_weights.shape[2]
    local_vch = points // stat_count // AVG
    fine = AVG // RADIX
    width = 2 * rows
    blocks = spectra_blocks(voltages, stat_count, local_vch)
    blocks = blocks.reshape(stat_count, local_vch, items * AVG, width)
    spread, gathered = exchange(blocks, beam_weights.reshape(width, beams_count), stat_count, time_count)
    now = lax.axis_index("tm").astype(jnp.int32).reshape(1)
    scale = 1.0 / (items * time_count * AVG)
    beams, vis = correlate(spread, gathered, now, scale, stat_count * rows // time_count)
    beams = beams.reshape(local_vch, items, RADIX, fine, 2, beams_count).transpose(0, 3, 2, 1, 4, 5)
    beams = beams.reshape(local_vch * AVG, items, 2, beams_count)
    vis = vis.reshape(vis.shape[0], local_vch, -1, 2, 128).transpose(0, 1, 3, 2, 4)
    return beams, vis.reshape(vis.shape[0], local_vch, 2, stat_count * rows)


def fits_tiles(mesh, voltages):
    _, inputs, spectra, points = voltages.shape
    rows = inputs // mesh.shape["stat"]
    mine = inputs // mesh.shape["tm"]
    share = points // mesh.shape["stat"]
    even = mesh.shape["stat"] & (mesh.shape["stat"] - 1) == 0 and mesh.shape["stat"] >= 4
    return even and 2 * rows == 128 and mine % 128 == 0 and share % AVG == 0 and spectra // mesh.shape["tm"] <= 4 and mesh.shape["tm"] <= 2


def solution(mesh):
    def whole(voltages, beam_weights):
        return jax.shard_map(
            fast_body if fits_tiles(mesh, voltages) else body,
            mesh=mesh,
            in_specs=(P(None, "stat", "tm", None), P(None, "stat", None)),
            out_specs=(P("stat", "tm", None, None), P("tm", "stat", None, None)),
            check_vma=False,
        )(voltages, beam_weights)

    return whole
```

```python
import functools
import math

import jax
import jax.numpy as jnp
import numpy as np
from jax import lax
from jax.experimental import pallas as pl
from jax.experimental.pallas import tpu as pltpu
from jax.sharding import PartitionSpec as P

NA = 16
NB = 256
AVG = 128


def dft_block(length):
    index = jnp.arange(length, dtype=jnp.int32)
    product = index[:, None] * index[None, :] % length
    angle = product.astype(jnp.float32) * (2.0 * math.pi / length)
    cosine = jnp.cos(angle)
    sine = jnp.sin(angle)
    return jnp.stack([jnp.stack([cosine, -sine]), jnp.stack([sine, cosine])])


def fine_spectra(voltages):
    block_inputs = voltages.shape[1]
    spectra_count = voltages.shape[2]
    signal = voltages.astype(jnp.float32).reshape(2, block_inputs, spectra_count, NA, NB)
    first = jnp.einsum("poak,pisab->osikb", dft_block(NA), signal, precision=lax.Precision.HIGH)
    outer_index = jnp.arange(NA, dtype=jnp.int32)
    inner_index = jnp.arange(NB, dtype=jnp.int32)
    rotation = (outer_index[:, None] * inner_index[None, :] % (NA * NB)).astype(jnp.float32) * (
        2.0 * math.pi / (NA * NB)
    )
    cos_twist = jnp.cos(rotation)
    sin_twist = jnp.sin(rotation)
    rotated = jnp.stack(
        [first[0] * cos_twist + first[1] * sin_twist, first[1] * cos_twist - first[0] * sin_twist]
    )
    final = jnp.einsum("osikb,ocbq->csiqk", rotated, dft_block(NB), precision=lax.Precision.HIGH)
    norm_factor = 1.0 / math.sqrt(NA * NB)
    return (
        (final * norm_factor).reshape(2, spectra_count, block_inputs, NA * NB).astype(jnp.bfloat16)
    )


def stack_weights(weights):
    return jnp.stack(
        [jnp.stack([weights[0], weights[1]], 1), jnp.stack([-weights[1], weights[0]], 1)], 0
    )


def body(voltages, beam_weights):
    stat_count = lax.axis_size("stat")
    time_count = lax.axis_size("tm")
    block_inputs = voltages.shape[1]
    spectra = fine_spectra(voltages)
    spectra_count = spectra.shape[1]
    channel_share = NA * NB // stat_count
    all_weights = lax.all_gather(beam_weights, "stat", axis=1, tiled=True)
    full_stack = stack_weights(all_weights)
    turned = lax.all_to_all(spectra, "stat", split_axis=3, concat_axis=2, tiled=True)
    item_count = turned.shape[1]

    def add_block(block_index, running):
        offset = (block_index * block_inputs).astype(jnp.int32)
        spec_block = lax.dynamic_slice_in_dim(turned, offset, block_inputs, 2)
        weight_block = lax.dynamic_slice_in_dim(full_stack, offset, block_inputs, 1)
        partial_value = jnp.einsum(
            "psic,piqb->csqb", spec_block, weight_block, preferred_element_type=jnp.float32
        )
        rounded = lax.optimization_barrier(partial_value.astype(jnp.bfloat16))
        return running + rounded.astype(jnp.float32)

    initial = jnp.zeros((turned.shape[3], item_count, 2, beam_weights.shape[2]), jnp.float32)
    beams = lax.fori_loop(0, stat_count, add_block, initial).astype(jnp.bfloat16)
    local_vch = channel_share // AVG
    scale = 1.0 / (spectra_count * time_count * AVG)
    split = turned.reshape(2, spectra_count, stat_count * block_inputs, local_vch, AVG)
    real_gram = jnp.einsum("psiva,psjva->ivj", split, split, preferred_element_type=jnp.float32)
    mixed = jnp.einsum("siva,sjva->ivj", split[1], split[0], preferred_element_type=jnp.float32)
    mixed = mixed - jnp.einsum(
        "siva,sjva->ivj", split[0], split[1], preferred_element_type=jnp.float32
    )
    visibilities = lax.psum_scatter(
        (jnp.stack([real_gram, mixed], axis=2) * scale).astype(jnp.bfloat16),
        "tm",
        scatter_dimension=0,
        tiled=True,
    ).astype(jnp.float32)
    return (beams, visibilities)

RADIX = 8


def dft_tables(points):
    inner = points // RADIX
    index = np.arange(inner)
    angle = 2.0 * np.pi * (index[:, None] * index[None, :] % inner) / inner
    scale = 1.0 / math.sqrt(points)
    matrix = np.concatenate([np.cos(angle), np.sin(angle)], 1) * scale
    turn = 2.0 * np.pi * (np.arange(RADIX)[:, None] * index[None, :]) / points
    return (
        jnp.asarray(matrix, jnp.bfloat16),
        jnp.asarray(np.cos(turn), jnp.float32),
        jnp.asarray(np.sin(turn), jnp.float32),
    )


def cadd(a, b):
    return a[0] + b[0], a[1] + b[1]


def csub(a, b):
    return a[0] - b[0], a[1] - b[1]


def times_minus_i(a):
    return a[1], -a[0]


def radix4(a):
    s02, d02 = cadd(a[0], a[2]), csub(a[0], a[2])
    s13, d13 = cadd(a[1], a[3]), times_minus_i(csub(a[1], a[3]))
    return [cadd(s02, s13), cadd(d02, d13), csub(s02, s13), csub(d02, d13)]


def radix8(a):
    even, odd = radix4(a[0::2]), radix4(a[1::2])
    root = math.sqrt(0.5)
    o1, o2, o3 = odd[1], times_minus_i(odd[2]), odd[3]
    o1 = ((o1[0] + o1[1]) * root, (o1[1] - o1[0]) * root)
    o3 = ((o3[1] - o3[0]) * root, (-o3[0] - o3[1]) * root)
    odd = [odd[0], o1, o2, o3]
    return [cadd(e, o) for e, o in zip(even, odd)] + [csub(e, o) for e, o in zip(even, odd)]


def fft_kernel(x_ref, m_ref, cos_ref, sin_ref, out_ref, mid):
    rows, points = x_ref.shape[2:]
    inner = points // RADIX
    chunk = 16

    @pl.loop(0, rows // chunk)
    def _(step):
        at = pl.ds(pl.multiple_of(step * chunk, chunk), chunk)
        low = pl.ds(pl.multiple_of(rows + step * chunk, chunk), chunk)
        for lane in range(0, inner, 128):
            parts = []
            for n1 in range(RADIX):
                cut = pl.ds(n1 * inner + lane, 128)
                parts.append(
                    (x_ref[0, 0, at, cut].astype(jnp.float32), x_ref[1, 0, at, cut].astype(jnp.float32))
                )
            for k1, (re, im) in enumerate(radix8(parts)):
                if k1:
                    c, s = cos_ref[k1:k1 + 1, lane:lane + 128], sin_ref[k1:k1 + 1, lane:lane + 128]
                    re, im = re * c + im * s, im * c - re * s
                re, im = re.astype(jnp.bfloat16), im.astype(jnp.bfloat16)
                left, right = pl.ds(lane, 128), pl.ds(inner + lane, 128)
                mid[k1, at, left] = re
                mid[k1, at, right] = im
                mid[k1, low, left] = im
                mid[k1, low, right] = -re

    width = 2 * rows
    for k1 in range(0, RADIX, 2):
        pair = mid[k1:k1 + 2].reshape(2 * width, 2 * inner)
        done = lax.dot_general(
            m_ref[...], pair, (((1,), (1,)), ((), ())), preferred_element_type=jnp.float32
        ).astype(jnp.bfloat16)
        for half in range(2):
            out_ref[:, :, 0, k1 + half] = done[:, half * width:(half + 1) * width].reshape(
                out_ref.shape[0], out_ref.shape[1], out_ref.shape[4], width
            )


def spectra_blocks(voltages, stat_count, local_vch):
    _, rows, items, points = voltages.shape
    inner = points // RADIX
    fine = AVG // RADIX
    matrix, cos_turn, sin_turn = dft_tables(points)
    whole = lambda shape: pl.BlockSpec(shape, lambda s: (0,) * len(shape))
    return pl.pallas_call(
        fft_kernel,
        grid=(items,),
        in_specs=[
            pl.BlockSpec((2, 1, rows, points), lambda s: (0, s, 0, 0)),
            whole(matrix.shape),
            whole(cos_turn.shape),
            whole(sin_turn.shape),
        ],
        out_specs=pl.BlockSpec(
            (stat_count, local_vch, 1, RADIX, fine, 2 * rows), lambda s: (0, 0, s, 0, 0, 0)
        ),
        out_shape=jax.ShapeDtypeStruct(
            (stat_count, local_vch, items, RADIX, fine, 2 * rows), jnp.bfloat16
        ),
        scratch_shapes=[pltpu.VMEM((RADIX, 2 * rows, 2 * inner), jnp.bfloat16)],
        name="fft",
    )(voltages.transpose(0, 2, 1, 3), matrix, cos_turn, sin_turn)


def send_order(count):
    near = []
    half = 1
    while half < count // 4:
        near += [(half, j) for j in range(half)]
        half *= 2
    far = [(count // 2, j) for j in range(count // 2)]
    middle = [(half, j) for j in range(half)] if half < count // 2 else []
    mixed = []
    while far or middle:
        mixed += far[:2] + middle[:1]
        far, middle = far[2:], middle[1:]
    return near + mixed


def exchange_kernel(stat_count, time_count, spec_ref, w_ref, y_ref, wg_ref, own, wown, loc, wloc,
                    send, recv, wsend, wrecv, fsend, frecv):
    me, now = lax.axis_index("stat"), lax.axis_index("tm")

    def place(time, source):
        return y_ref.at[time, source]

    pieces = spec_ref.shape[1]

    def forward(source, src, k, part):
        made = []
        for j in range(1, time_count):
            copy = pltpu.make_async_remote_copy(
                src_ref=src.at[part], dst_ref=place(now, source).at[part],
                send_sem=fsend.at[j, k * pieces + part], recv_sem=frecv.at[j, k * pieces + part],
                device_id={"tm": lax.rem(now + j, time_count)}, device_id_type=pl.DeviceIdType.MESH)
            copy.start()
            made.append(copy)
        return made

    barrier = pltpu.get_barrier_semaphore()
    for k in range(1, stat_count):
        pl.semaphore_signal(barrier, inc=1, device_id={"stat": lax.rem(me + k, stat_count)},
                            device_id_type=pl.DeviceIdType.MESH)
    for j in range(1, time_count):
        pl.semaphore_signal(barrier, inc=1, device_id={"tm": lax.rem(now + j, time_count)},
                            device_id_type=pl.DeviceIdType.MESH)
    pl.semaphore_wait(barrier, stat_count + time_count - 2)

    order = send_order(stat_count)

    def partner(k, sign):
        half = k[0]
        other = me // half + 1 - 2 * lax.rem(me // half, 2)
        return other * half + lax.rem(lax.rem(me, half) + half + sign * k[1], half)

    sends = [(partner(k, 1), slot) for slot, k in enumerate(order, 1)]
    sources = [(partner(k, -1), slot) for slot, k in enumerate(order, 1)]

    def to(src, dst, there, out_sem, in_sem):
        return pltpu.make_async_remote_copy(
            src_ref=src, dst_ref=dst, send_sem=out_sem, recv_sem=in_sem,
            device_id={"stat": there}, device_id_type=pl.DeviceIdType.MESH)

    levels = []
    reach = stat_count // 2
    while reach:
        levels.append(reach)
        reach //= 2

    def level_copies(level):
        reach = levels[level]
        period = 2 * reach
        other = partner((reach, 0), 1)
        made = []
        for turn in range(stat_count // period):
            block = lax.rem(me, period) + period * turn
            index = stat_count // period + turn
            made.append(to(
                wg_ref.at[block] if level else w_ref, wg_ref.at[block], other,
                wsend.at[index], wrecv.at[index]))
        return made

    def start_level(level):
        started.append(level_copies(level))
        for copy in started[-1]:
            copy.start()

    def end_level(level):
        for copy in started[level]:
            copy.wait_recv()

    copies, started = [], []
    wtake = pltpu.make_async_copy(w_ref, wown, wloc)
    wtake.start()
    start_level(0)
    wtake.wait()
    wput = pltpu.make_async_copy(wown, wg_ref.at[me], wloc)
    wput.start()
    early = 5
    for number, (there, slot) in enumerate(sends):
        if number == early:
            wput.wait()
            end_level(0)
            start_level(1)
        for part in range(pieces):
            copies.append(to(
                spec_ref.at[there, part], place(now, me).at[part], there,
                send.at[number * pieces + part], recv.at[slot * pieces + part]))
            copies[-1].start()
    made = []
    for part in range(pieces):
        made += forward(me, spec_ref.at[me], 0, part)
    take = pltpu.make_async_copy(spec_ref.at[me], own, loc)
    take.start()
    take.wait()
    put = pltpu.make_async_copy(own, place(now, me), loc)
    put.start()
    for number, (source, slot) in enumerate(sources):
        if number % 4 == 3 and len(started) < len(levels):
            end_level(len(started) - 1)
            start_level(len(started))
        for part in range(pieces):
            to(spec_ref.at[source, part], place(now, source).at[part], source,
               send.at[0], recv.at[slot * pieces + part]).wait_recv()
            made += forward(source, place(now, source), slot, part)
    while len(started) < len(levels):
        end_level(len(started) - 1)
        start_level(len(started))
    end_level(len(levels) - 1)
    for copy in copies:
        copy.wait_send()
    for level in started:
        for copy in level:
            copy.wait_send()
    put.wait()
    for copy in made:
        copy.wait()


def exchange(blocks, weights, stat_count, time_count):
    dma = pltpu.SemaphoreType.DMA
    peers = dma((stat_count,))
    parts = stat_count * blocks.shape[1]
    return pl.pallas_call(
        functools.partial(exchange_kernel, stat_count, time_count),
        in_specs=[pl.BlockSpec(memory_space=pl.ANY)] * 2,
        out_specs=[pl.BlockSpec(memory_space=pl.ANY)] * 2,
        out_shape=[
            jax.ShapeDtypeStruct((time_count,) + blocks.shape, blocks.dtype),
            jax.ShapeDtypeStruct((stat_count,) + weights.shape, weights.dtype),
        ],
        scratch_shapes=[
            pltpu.VMEM(blocks.shape[1:], blocks.dtype), pltpu.VMEM(weights.shape, weights.dtype),
            dma, dma, dma((parts,)), dma((parts,)), peers, peers,
            dma((time_count, parts)), dma((time_count, parts)),
        ],
        compiler_params=pltpu.CompilerParams(collective_id=0, has_side_effects=True),
        name="exchange",
    )(blocks, weights)


def correlate_kernel(scale, now_ref, y_ref, w_ref, beam_ref, vis_ref, cols, left, stacked):
    now = now_ref[0]
    times, sources, _, depth, width = y_ref.shape
    total = times * depth
    half = width // 2
    inputs = sources * half
    mine = vis_ref.shape[0]
    groups = vis_ref.shape[2]
    flat = vis_ref.reshape(mine * groups, 128)
    beams = w_ref.shape[2]
    for time in range(times):
        for source in range(0, sources, 2):
            a = y_ref[time, source, 0]
            b = y_ref[time, source + 1, 0]
            out = pl.ds(source * half, width)
            cols[pl.ds(time * depth, depth), out] = jnp.concatenate([a[:, :half], b[:, :half]], 1)
            cols[pl.ds(total + time * depth, depth), out] = jnp.concatenate([a[:, half:], b[:, half:]], 1)
    for tile in range(0, mine, 128):
        at = pl.ds(pl.multiple_of(now * mine + tile, 128), 128)
        re = (cols[pl.ds(0, total), at]).T
        im = (cols[pl.ds(total, total), at]).T
        left[pl.ds(tile, 128), pl.ds(0, total)] = re
        left[pl.ds(tile, 128), pl.ds(total, total)] = im
        left[pl.ds(mine + tile, 128), pl.ds(0, total)] = im
        left[pl.ds(mine + tile, 128), pl.ds(total, total)] = -re
    block = 256

    @pl.loop(0, inputs // block)
    def _(n):
        at = pl.ds(pl.multiple_of(n * block, block), block)
        for q in range(2):
            value = scale * jnp.dot(
                left[pl.ds(q * mine, mine), :], cols[:, at], preferred_element_type=jnp.float32)
            for part in range(block // 128):
                row = (n * (block // 128) + part) * 2 + q
                flat[pl.ds(row, mine, stride=groups), :] = value[:, part * 128:part * 128 + 128]

    for source in range(sources):
        upper = pl.ds(source * half, half)
        lower = pl.ds(inputs + source * half, half)
        stacked[upper, pl.ds(0, beams)] = w_ref[source, :half]
        stacked[upper, pl.ds(beams, beams)] = w_ref[source, half:]
        stacked[lower, pl.ds(0, beams)] = -w_ref[source, half:]
        stacked[lower, pl.ds(beams, beams)] = w_ref[source, :half]
    shift = pl.multiple_of(now * depth, depth)
    real = jnp.dot(
        cols[pl.ds(shift, depth), :], stacked[pl.ds(0, inputs), :], preferred_element_type=jnp.float32)
    imag = jnp.dot(
        cols[pl.ds(total + shift, depth), :], stacked[pl.ds(inputs, inputs), :],
        preferred_element_type=jnp.float32)
    beam_ref[0] = (real + imag).astype(jnp.bfloat16)


def correlate(spread, weights, now, scale, mine):
    times, sources, vch, depth, width = spread.shape
    lanes = sources * width
    wide = 2 * weights.shape[2]
    groups = lanes // 128
    inputs = lanes // 2
    return pl.pallas_call(
        functools.partial(correlate_kernel, scale),
        grid_spec=pltpu.PrefetchScalarGridSpec(
            num_scalar_prefetch=1,
            grid=(vch,),
            in_specs=[
                pl.BlockSpec((times, sources, 1, depth, width), lambda v, t: (0, 0, v, 0, 0)),
                pl.BlockSpec(weights.shape, lambda v, t: (0, 0, 0)),
            ],
            out_specs=[
                pl.BlockSpec((1, depth, wide), lambda v, t: (v, 0, 0)),
                pl.BlockSpec((mine, 1, groups, 128), lambda v, t: (0, v, 0, 0)),
            ],
            scratch_shapes=[
                pltpu.VMEM((2 * times * depth, inputs), jnp.bfloat16),
                pltpu.VMEM((2 * mine, 2 * times * depth), jnp.bfloat16),
                pltpu.VMEM((lanes, wide), jnp.bfloat16),
            ],
        ),
        out_shape=[
            jax.ShapeDtypeStruct((vch, depth, wide), jnp.bfloat16),
            jax.ShapeDtypeStruct((mine, vch, groups, 128), jnp.float32),
        ],
        name="correlate",
    )(now, spread, weights)


def fast_body(voltages, beam_weights):
    stat_count = lax.axis_size("stat")
    time_count = lax.axis_size("tm")
    _, rows, items, points = voltages.shape
    beams_count = beam_weights.shape[2]
    local_vch = points // stat_count // AVG
    fine = AVG // RADIX
    width = 2 * rows
    blocks = spectra_blocks(voltages, stat_count, local_vch)
    blocks = blocks.reshape(stat_count, local_vch, items * AVG, width)
    spread, gathered = exchange(blocks, beam_weights.reshape(width, beams_count), stat_count, time_count)
    now = lax.axis_index("tm").astype(jnp.int32).reshape(1)
    scale = 1.0 / (items * time_count * AVG)
    beams, vis = correlate(spread, gathered, now, scale, stat_count * rows // time_count)
    beams = beams.reshape(local_vch, items, RADIX, fine, 2, beams_count).transpose(0, 3, 2, 1, 4, 5)
    beams = beams.reshape(local_vch * AVG, items, 2, beams_count)
    vis = vis.reshape(vis.shape[0], local_vch, -1, 2, 128).transpose(0, 1, 3, 2, 4)
    return beams, vis.reshape(vis.shape[0], local_vch, 2, stat_count * rows)


def fits_tiles(mesh, voltages):
    _, inputs, spectra, points = voltages.shape
    rows = inputs // mesh.shape["stat"]
    mine = inputs // mesh.shape["tm"]
    share = points // mesh.shape["stat"]
    even = mesh.shape["stat"] & (mesh.shape["stat"] - 1) == 0 and mesh.shape["stat"] >= 8
    return even and 2 * rows == 128 and mine % 128 == 0 and share % AVG == 0 and spectra // mesh.shape["tm"] <= 4 and mesh.shape["tm"] <= 2


def solution(mesh):
    def whole(voltages, beam_weights):
        return jax.shard_map(
            fast_body if fits_tiles(mesh, voltages) else body,
            mesh=mesh,
            in_specs=(P(None, "stat", "tm", None), P(None, "stat", None)),
            out_specs=(P("stat", "tm", None, None), P("tm", "stat", None, None)),
            check_vma=False,
        )(voltages, beam_weights)

    return whole
```
